32 devices in a mesh: width: 4 (over z), token: 4 (over y, core), query: 2 (over x).
Axes of the slice: x: 2, y: 2, z: 4, core: 2. Of those that a mesh axis runs over, the one named last changes fastest.
Arguments:
- layer_inputs: bfloat16 [1536, 8192], P(('token', 'query'), 'width'), may hold values from -20 to 20
- out_grads: bfloat16 [1536, 8192], P(('token', 'query'), 'width'), may hold values from -20 to 20
- basis_in: bfloat16 [8192, 8192], P(None, 'width'), may hold values from -0.125 to 0.125
- basis_out: bfloat16 [8192, 8192], P(None, 'width'), may hold values from -0.125 to 0.125
- query_in: bfloat16 [256, 32, 8192], P('query', None, 'width'), may hold values from -0.03125 to 0.03125
- query_out: bfloat16 [256, 32, 8192], P('query', None, 'width'), may hold values from -0.03125 to 0.03125
Outputs:
- scores: float32 [256, 1536], P('query', 'token')
The draws below stay inside these ranges and needn't reach their ends.
All inputs are finite; a program needn't handle non-finite values.
Results may differ from the reference program's by a relative error of at most 0.0003.
Values may be sent and summed in bfloat16 or wider, within the bound.
No kernel may reach another device: no remote copies, remote signals or barrier semaphores. Data moves between devices by JAX's collectives and lax.ppermute only.
A program may use at most 192 MiB of HBM per device.

```python
import math
import jax
import jax.numpy as jnp
from jax import lax

D = 8192
RANK = 32
TOKENS = 1536
QUERIES = 256


def activation_draw(key, salt):
    first = jax.random.fold_in(jax.random.fold_in(key, salt), 0)
    base = jnp.clip(jax.random.normal(first, (TOKENS, D), jnp.float32), -4.0, 4.0)
    position = jnp.arange(TOKENS, dtype=jnp.float32) / TOKENS
    factor = 0.6 + 1.2 * position
    return (base * factor[:, None]).astype(jnp.bfloat16)


def basis_draw(key, salt):
    first, second = jax.random.split(jax.random.fold_in(key, salt))
    base = jnp.clip(jax.random.normal(first, (D, D), jnp.float32), -4.0, 4.0)
    column_scale = jnp.exp(jax.random.uniform(second, (D,), jnp.float32, math.log(0.3), math.log(3.0)))
    values = base * column_scale[None, :] / math.sqrt(D)
    return jnp.clip(values, -0.125, 0.125).astype(jnp.bfloat16)


def draw_layer_inputs(key, part):
    return activation_draw(key, 11)


def draw_out_grads(key, part):
    return activation_draw(key, 23)


def draw_basis_in(key, part):
    return basis_draw(key, 37)


def draw_basis_out(key, part):
    return basis_draw(key, 41)


def steps_of(own_key, extent, cuts, smallest, high):
    gain = 1.0
    for axis_at, blocks in cuts:
        steps = jax.random.uniform(jax.random.fold_in(jax.random.fold_in(own_key, 6), axis_at), (blocks,), jnp.float32, smallest / len(cuts), high / len(cuts))
        gain = gain * jnp.repeat(jnp.exp(steps), extent[axis_at] // blocks).reshape((-1,) + (1,) * (len(extent) - 1 - axis_at))
    return gain


def scatter_about(own_key, dims, width, reach, cuts=(), kind=jnp.bfloat16):
    entries = jax.random.normal(own_key, dims, jnp.float32) * width
    if len(cuts) > 0:
        entries = steps_of(own_key, dims, cuts, -0.22, 0.18) * entries
    return jnp.clip(entries, min=-reach, max=reach).astype(kind)


def setup_inputs(seed: int = 0) -> dict:
    seeds = jax.random.split(jax.random.key(seed), 7)
    layer_inputs = draw_layer_inputs(jax.random.fold_in(seeds[6], 71), 0)
    out_grads = draw_out_grads(jax.random.fold_in(seeds[6], 71), 0)
    basis_in = draw_basis_in(jax.random.fold_in(seeds[6], 71), 0)
    basis_out = draw_basis_out(jax.random.fold_in(seeds[6], 71), 0)
    query_in = scatter_about(seeds[4], (QUERIES, RANK, D), (4 * D) ** -0.5, 0.03125, ((0, 2), (2, 4)))
    query_out = scatter_about(seeds[5], (QUERIES, RANK, D), (4 * D) ** -0.5, 0.03125, ((0, 2), (2, 4)))
    return {"layer_inputs": layer_inputs, "out_grads": out_grads, "basis_in": basis_in, "basis_out": basis_out, "query_in": query_in, "query_out": query_out}


damping = 0.1


def reference(layer_inputs, out_grads, basis_in, basis_out, query_in, query_out):
    rotated_in = jnp.dot(layer_inputs, basis_in, preferred_element_type=jnp.float32)
    rotated_out = jnp.dot(out_grads, basis_out, preferred_element_type=jnp.float32)
    eigen_in = jnp.sum(rotated_in * rotated_in, axis=0) / TOKENS
    eigen_out = jnp.sum(rotated_out * rotated_out, axis=0) / TOKENS
    scaled_in = rotated_in / (eigen_in + damping)
    scaled_out = rotated_out / (eigen_out + damping)
    flat_in = query_in.reshape(QUERIES * RANK, D).astype(jnp.float32)
    flat_out = query_out.reshape(QUERIES * RANK, D).astype(jnp.float32)
    pair_in = jnp.dot(flat_in, scaled_in.T, precision=lax.Precision.HIGHEST, preferred_element_type=jnp.float32)
    pair_out = jnp.dot(flat_out, scaled_out.T, precision=lax.Precision.HIGHEST, preferred_element_type=jnp.float32)
    return (pair_in * pair_out).reshape(QUERIES, RANK, TOKENS).sum(axis=1)
```

```python
import functools

import jax
import jax.numpy as jnp
from jax import lax
from jax.experimental import pallas as pl
from jax.experimental.pallas import tpu as pltpu
from jax.sharding import PartitionSpec as P

damping = 0.1
reach = 172.0
floor = 1e-30
scale_rows = 16
row_block = 512
basis_block = 512
chunks_in = 2
chunks_out = 2


def swap_pairs(count):
    even = [(i, i ^ 1) for i in range(count)]
    odd = [(0, 0), (count - 1, count - 1)] + [(i, i + 1 if i % 2 else i - 1) for i in range(1, count - 1)]
    return even, odd


def shift_pairs(count, by):
    return [(i, (i + by) % count) for i in range(count)]


def rotate_step(acc, chunks, basis, sources, valid, last):
    tokens, depth = chunks[0].shape
    cols = basis.shape[1]
    bk = min(basis_block, depth)
    nk = depth // bk
    n = len(chunks)
    if n == 1:
        base = sources * nk
        stride = jnp.ones((1,), jnp.int32)
    else:
        first = jnp.where(valid[0] > 0, sources[0] * nk, sources[1] * nk)
        second = jnp.where(valid[1] > 0, sources[1] * nk, sources[0] * nk + nk - 1)
        base = jnp.stack([first, second])
        stride = valid
    has_acc = acc is not None

    def body(base_ref, stride_ref, valid_ref, *refs):
        chunk_refs = refs[:n]
        basis_ref = refs[n]
        acc_ref = refs[n + 1] if has_acc else None
        out_ref = refs[n + 1 + has_acc]
        c, k = pl.program_id(0), pl.program_id(1)

        @pl.when((c == 0) & (k == 0))
        def _():
            if has_acc:
                out_ref[...] = acc_ref[...]
            else:
                out_ref[...] = jnp.zeros_like(out_ref)

        for i in range(n):
            @pl.when((c == i) & (valid_ref[i] > 0))
            def _():
                out_ref[...] += jnp.dot(chunk_refs[i][...], basis_ref[...], preferred_element_type=jnp.float32)

        if last:
            @pl.when((c == n - 1) & (k == nk - 1))
            def _():
                total = out_ref[...]
                refs[-1][...] = jnp.sum(total * total, axis=0, keepdims=True)

    whole = pl.BlockSpec((tokens, cols), lambda c, k, b, s, v: (0, 0))
    in_specs = [pl.BlockSpec((tokens, bk), lambda c, k, b, s, v: (0, k)) for _ in range(n)]
    in_specs.append(pl.BlockSpec((bk, cols), lambda c, k, b, s, v: (b[c] + s[c] * k, 0)))
    operands = [*chunks, basis]
    if has_acc:
        in_specs.append(whole)
        operands.append(acc)
    out_shape = [jax.ShapeDtypeStruct((tokens, cols), jnp.float32)]
    out_specs = [whole]
    if last:
        out_shape.append(jax.ShapeDtypeStruct((1, cols), jnp.float32))
        out_specs.append(pl.BlockSpec((1, cols), lambda c, k, b, s, v: (0, 0)))
    out = pl.pallas_call(
        body,
        out_shape=out_shape,
        grid_spec=pltpu.PrefetchScalarGridSpec(
            num_scalar_prefetch=3, grid=(n, nk), in_specs=in_specs, out_specs=out_specs
        ),
        compiler_params=pltpu.CompilerParams(dimension_semantics=("arbitrary", "arbitrary")),
        cost_estimate=pl.CostEstimate(
            flops=2 * tokens * depth * cols, transcendentals=0, bytes_accessed=depth * cols * 2 + tokens * cols * 8
        ),
        name="rotate",
    )(base, stride, valid, *operands)
    return out if last else out[0]


def split_scaled(rotated, squares, slots, total_tokens):
    n = len(rotated)
    tokens, cols = rotated[0].shape
    bt = tokens // 4 if tokens % 64 == 0 else tokens
    nb = tokens // bt

    def body(slot_ref, squares_ref, *refs):
        out_ref = refs[-1]
        gain = squares_ref[...] / total_tokens + damping
        for i in range(n):
            @pl.when(pl.program_id(0) == i)
            def _():
                scaled = refs[i][...] / gain
                head = scaled.astype(jnp.bfloat16)
                out_ref[0] = head
                out_ref[1] = (scaled - head.astype(jnp.float32)).astype(jnp.bfloat16)

    in_specs = [pl.BlockSpec((1, cols), lambda g, b, s: (0, 0))]
    for i in range(n):
        in_specs.append(pl.BlockSpec((bt, cols), lambda g, b, s, i=i: (jnp.where(g == i, b, jnp.where(g < i, 0, nb - 1)), 0)))
    return pl.pallas_call(
        body,
        out_shape=jax.ShapeDtypeStruct((2, n * tokens, cols), jnp.bfloat16),
        grid_spec=pltpu.PrefetchScalarGridSpec(
            num_scalar_prefetch=1,
            grid=(n, nb),
            in_specs=in_specs,
            out_specs=pl.BlockSpec((2, bt, cols), lambda g, b, s: (0, s[g] * nb + b, 0)),
        ),
        compiler_params=pltpu.CompilerParams(dimension_semantics=("arbitrary", "arbitrary")),
        cost_estimate=pl.CostEstimate(
            flops=4 * n * tokens * cols, transcendentals=0, bytes_accessed=8 * n * tokens * cols
        ),
        name="split",
    )(slots, squares, *rotated)


def pair_step(rows, scaled, received, starts, length, block, mode, other=None, rank_count=None):
    depth = rows.shape[1]
    group = scaled.shape[1]
    nb = length // block
    n = len(received)

    def body(start_ref, row_ref, scaled_ref, *refs):
        both = scaled_ref[...].reshape(2 * group, depth)
        product = lax.dot_general(
            row_ref[...], both, (((1,), (1,)), ((), ())), preferred_element_type=jnp.float32
        )
        total = product[:, :group] + product[:, group:]
        for i in range(n):
            code = refs[i][:block, :].astype(jnp.float32)
            top = refs[i][block : block + 1, :].astype(jnp.float32)
            size = (jnp.log(jnp.abs(code)) + reach / 2) * (top * (1.0 / reach))
            total = total + jnp.where(code < 0, -size, size)
        out_ref = refs[-1]
        if mode == "code":
            top = jnp.max(jnp.abs(total), axis=0, keepdims=True)
            top = jnp.maximum(top * (1 + 2.0**-7), floor).astype(jnp.bfloat16)
            size = jnp.exp(jnp.abs(total) * (reach / top.astype(jnp.float32)) - reach / 2)
            out_ref[:block, :] = jnp.where(total < 0, -size, size).astype(jnp.bfloat16)
            out_ref[block:, :] = jnp.broadcast_to(top, (scale_rows, group))
        elif mode == "plain":
            out_ref[...] = total
        else:
            joined = total * refs[n][...]
            out_ref[...] = jnp.sum(joined.reshape(block // rank_count, rank_count, group), axis=1)

    in_specs = [
        pl.BlockSpec((block, depth), lambda b, s: (s[0] + b, 0)),
        pl.BlockSpec((2, group, depth), lambda b, s: (0, 0, 0), pipeline_mode=pl.Buffered(1)),
    ]
    for i in range(n):
        in_specs.append(pl.BlockSpec((block + scale_rows, group), lambda b, s, i=i: (s[1 + i] + b, 0)))
    operands = [rows, scaled, *received]
    if mode == "code":
        out_shape = jax.ShapeDtypeStruct((nb * (block + scale_rows), group), jnp.bfloat16)
        out_spec = pl.BlockSpec((block + scale_rows, group), lambda b, s: (b, 0))
    elif mode == "plain":
        out_shape = jax.ShapeDtypeStruct((length, group), jnp.float32)
        out_spec = pl.BlockSpec((block, group), lambda b, s: (b, 0))
    else:
        in_specs.append(pl.BlockSpec((block, group), lambda b, s: (b, 0)))
        operands.append(other)
        out_shape = jax.ShapeDtypeStruct((length // rank_count, group), jnp.float32)
        out_spec = pl.BlockSpec((block // rank_count, group), lambda b, s: (b, 0))
    return pl.pallas_call(
        body,
        out_shape=out_shape,
        grid_spec=pltpu.PrefetchScalarGridSpec(
            num_scalar_prefetch=1, grid=(nb,), in_specs=in_specs, out_specs=out_spec
        ),
        compiler_params=pltpu.CompilerParams(dimension_semantics=("arbitrary",)),
        cost_estimate=pl.CostEstimate(
            flops=4 * length * depth * group,
            transcendentals=2 * length * group,
            bytes_accessed=length * depth * 2 + 2 * group * depth * 2,
        ),
        name="pair_" + mode,
    )(starts, *operands)


def reduce_pairs(rows, scaled, first_row, length, width, others=None, rank_count=None):
    place = lax.axis_index("width")
    block = min(row_block, length // width)
    lo = jnp.int32(first_row // block)
    count = length // block
    received, kept_from = [], []
    step = 1
    while step < width:
        count //= 2
        upper = (place // step) % 2
        send_from = lo + (1 - upper) * count
        lo = lo + upper * count
        starts = jnp.stack([send_from] + [send_from - k for k in kept_from])
        code = pair_step(rows, scaled, received, starts, count * block, block, "code")
        received = received + [lax.ppermute(code, "width", [(i, i ^ step) for i in range(width)])]
        kept_from = kept_from + [lo]
        step *= 2
    starts = jnp.stack([lo] + [lo - k for k in kept_from])
    mode = "plain" if others is None else "joined"
    return pair_step(rows, scaled, received, starts, count * block, block, mode, others, rank_count)


def gather_rotate(own, basis, width):
    place = lax.axis_index("width")
    even, odd = swap_pairs(width)
    is_even = place % 2 == 0
    one = jnp.ones((1,), jnp.int32)
    acc = rotate_step(None, [own], basis, place[None].astype(jnp.int32), one, width == 1)
    send_even, send_odd = own, own
    for distance in range(1, width):
        last = distance == width - 1
        got_even = lax.ppermute(send_even, "width", even)
        right, left = place + distance, place - distance
        from_even = jnp.where(is_even, right, left)
        from_odd = jnp.where(is_even, left, right)
        if last:
            chunks, sources = [got_even], from_even[None]
        else:
            got_odd = lax.ppermute(send_odd, "width", odd)
            chunks, sources = [got_even, got_odd], jnp.stack([from_even, from_odd])
            send_even, send_odd = got_odd, got_even
        valid = ((sources >= 0) & (sources < width)).astype(jnp.int32)
        acc = rotate_step(acc, chunks, basis, jnp.clip(sources, 0, width - 1).astype(jnp.int32), valid, last)
    return acc


def sum_over(x, axis):
    count = lax.axis_size(axis)
    total = x
    for by in range(1, count):
        total = total + lax.ppermute(x, axis, shift_pairs(count, by))
    return total


def scaled_group(rotated, squares, total_tokens):
    count = lax.axis_size("query")
    place = lax.axis_index("query")
    sources = [rotated] + [lax.ppermute(rotated, "query", shift_pairs(count, by)) for by in range(1, count)]
    squares = sum_over(sum_over(squares, "token"), "query")
    slots = jnp.stack([(place - by) % count for by in range(count)]).astype(jnp.int32)
    return split_scaled(sources, squares, slots, total_tokens)


def on_device(layer_inputs, out_grads, basis_in, basis_out, query_in, query_out):
    width = lax.axis_size("width")
    place = lax.axis_index("width")
    total_tokens = layer_inputs.shape[0] * lax.axis_size("token") * lax.axis_size("query")
    queries, rank_count, width_cols = query_in.shape
    rows_in = query_in.reshape(-1, width_cols)
    rows_out = query_out.reshape(-1, width_cols)

    rotated_in, squares_in = gather_rotate(layer_inputs, basis_in, width)
    rotated_out, squares_out = gather_rotate(out_grads, basis_out, width)
    scaled_in = scaled_group(rotated_in, squares_in, total_tokens)
    scaled_out = scaled_group(rotated_out, squares_out, total_tokens)

    length = rows_in.shape[0] // chunks_in
    pairs_in = [reduce_pairs(rows_in, scaled_in, c * length, length, width) for c in range(chunks_in)]
    scores = jnp.stack(
        [
            reduce_pairs(rows_out, scaled_out, c * length, length, width, pairs_in[c], rank_count)
            for c in range(chunks_in)
        ]
    )
    step = width // 2
    while step:
        got = lax.ppermute(scores, "width", [(i, i ^ step) for i in range(width)])
        upper = (place // step) % 2
        scores = jnp.where(
            upper == 0, jnp.concatenate([scores, got], axis=1), jnp.concatenate([got, scores], axis=1)
        )
        step //= 2
    return scores.reshape(queries, scores.shape[-1])


def solution(mesh):
    return jax.shard_map(
        on_device,
        mesh=mesh,
        in_specs=(
            P(("token", "query"), "width"),
            P(("token", "query"), "width"),
            P(None, "width"),
            P(None, "width"),
            P("query", None, "width"),
            P("query", None, "width"),
        ),
        out_specs=P("query", "token"),
        check_vma=False,
    )
```

```python
import functools

import jax
import jax.numpy as jnp
from jax import lax
from jax.experimental import pallas as pl
from jax.experimental.pallas import tpu as pltpu
from jax.sharding import PartitionSpec as P

damping = 0.1
reach = 172.0
floor = 1e-30
scale_rows = 16
row_block = 512
basis_block = 1024
basis_streams = 2
split_block = 512
chunks = 2
parts_in = 2
parts_out = 1


def swap_pairs(count):
    even = [(i, i ^ 1) for i in range(count)]
    odd = [(0, 0), (count - 1, count - 1)] + [(i, i + 1 if i % 2 else i - 1) for i in range(1, count - 1)]
    return even, odd


def shift_pairs(count, by):
    return [(i, (i + by) % count) for i in range(count)]


def line_sources(width, place):
    got = []
    for distance in range(1, width):
        right, left = place + distance, place - distance
        pair = (right, left) if place % 2 == 0 else (left, right)
        got += [pair[0]] if distance == width - 1 else list(pair)
    return [source if 0 <= source < width else None for source in got]


def rotate_plan(width, nk):
    rows = []
    for place in range(width):
        sources = [place] + line_sources(width, place)
        blocks, hold = [], 0
        for source in sources:
            for k in range(nk):
                hold = hold if source is None else source * nk + k
                blocks.append(hold)
        rows.append(blocks + [int(source is not None) for source in sources])
    return rows


def rotate_step(acc, first, buffers, basis, plan, count, last):
    tokens = sum(part.shape[0] for part in buffers[0])
    depth = buffers[0][0].shape[1]
    cols = basis.shape[1]
    bk = min(basis_block, depth)
    nk = depth // bk
    n = len(buffers)
    parts = [part for buffer in buffers for part in buffer]
    has_acc = acc is not None

    def body(plan_ref, *refs):
        part_refs = list(refs[: len(parts)])
        refs = refs[len(parts) :]
        basis_refs = refs[:basis_streams]
        acc_ref = refs[basis_streams] if has_acc else None
        out_refs = refs[basis_streams + has_acc :]
        out_ref = out_refs[0]
        c, k = pl.program_id(0), pl.program_id(1)

        @pl.when((c == 0) & (k == 0))
        def _():
            if has_acc:
                out_ref[...] = acc_ref[...]
            else:
                out_ref[...] = jnp.zeros_like(out_ref)

        for i in range(n):
            mine = [part_refs.pop(0) for _ in buffers[i]]

            @pl.when((c == i) & (plan_ref[count * nk + first + i] > 0))
            def _():
                chunk = mine[0][...] if len(mine) == 1 else jnp.concatenate([ref[...] for ref in mine], axis=0)
                piece = bk // basis_streams
                total = out_ref[...]
                for j in range(basis_streams):
                    total += jnp.dot(
                        chunk[:, j * piece : (j + 1) * piece], basis_refs[j][...], preferred_element_type=jnp.float32
                    )
                out_ref[...] = total

        if last:
            @pl.when((c == n - 1) & (k == nk - 1))
            def _():
                total = out_ref[...]
                out_refs[1][...] = jnp.sum(total * total, axis=0, keepdims=True)
                encode(total, out_refs[2])

    whole = pl.BlockSpec((tokens, cols), lambda c, k, s: (0, 0))
    in_specs = []
    for i in range(n):
        for part in buffers[i]:
            in_specs.append(
                pl.BlockSpec(
                    (part.shape[0], bk),
                    lambda c, k, s, i=i: (0, jnp.where(c == i, k, jnp.where(c < i, 0, nk - 1))),
                )
            )
    for j in range(basis_streams):
        in_specs.append(
            pl.BlockSpec(
                (bk // basis_streams, cols),
                lambda c, k, s, j=j: (s[(first + c) * nk + k] * basis_streams + j, 0),
            )
        )
    operands = [*parts, *[basis] * basis_streams]
    if has_acc:
        in_specs.append(whole)
        operands.append(acc)
    out_shape = [jax.ShapeDtypeStruct((tokens, cols), jnp.float32)]
    out_specs = [whole]
    if last:
        out_shape.append(jax.ShapeDtypeStruct((1, cols), jnp.float32))
        out_specs.append(pl.BlockSpec((1, cols), lambda c, k, s: (0, 0)))
        out_shape.append(jax.ShapeDtypeStruct((tokens + scale_rows, cols), jnp.bfloat16))
        out_specs.append(pl.BlockSpec((tokens + scale_rows, cols), lambda c, k, s: (0, 0)))
    out = pl.pallas_call(
        body,
        out_shape=out_shape,
        grid_spec=pltpu.PrefetchScalarGridSpec(
            num_scalar_prefetch=1, grid=(n, nk), in_specs=in_specs, out_specs=out_specs
        ),
        compiler_params=pltpu.CompilerParams(dimension_semantics=("arbitrary", "arbitrary")),
        cost_estimate=pl.CostEstimate(
            flops=4 * tokens * depth * cols, transcendentals=0, bytes_accessed=2 * depth * cols * 2 + tokens * cols * 8
        ),
        name="rotate",
    )(plan, *operands)
    return out if last else out[0]


def encode(value, out_ref):
    count = value.shape[0]
    top = jnp.max(jnp.abs(value), axis=0, keepdims=True)
    top = jnp.maximum(top * (1 + 2.0**-7), floor).astype(jnp.bfloat16)
    size = jnp.exp(jnp.abs(value) * (reach / top.astype(jnp.float32)) - reach / 2)
    out_ref[:count, :] = jnp.where(value < 0, -size, size).astype(jnp.bfloat16)
    out_ref[count:, :] = jnp.broadcast_to(top, (scale_rows, value.shape[1]))


def decode(ref):
    count = ref.shape[0] - scale_rows
    code = ref[:count, :].astype(jnp.float32)
    top = ref[count : count + 1, :].astype(jnp.float32)
    size = (jnp.log(jnp.abs(code)) + reach / 2) * (top * (1.0 / reach))
    return jnp.where(code < 0, -size, size)


def split_scaled(rotated, codes, squares, place, total_tokens):
    n = 1 + len(codes)
    tokens, cols = rotated.shape
    bc = min(split_block, cols)

    def body(place_ref, squares_ref, *refs):
        out_ref = refs[-1]
        gain = 1.0 / (squares_ref[...] / total_tokens + damping)
        for by in range(n):
            scaled = (refs[0][...] if by == 0 else decode(refs[by])) * gain
            head = scaled.astype(jnp.bfloat16)
            slot = lax.rem(place_ref[0] + (n - by), n) * tokens
            rows = pl.ds(pl.multiple_of(slot, tokens), tokens)
            out_ref[0, rows, :] = head
            out_ref[1, rows, :] = (scaled - head.astype(jnp.float32)).astype(jnp.bfloat16)

    in_specs = [pl.BlockSpec((1, bc), lambda b, s: (0, b)), pl.BlockSpec((tokens, bc), lambda b, s: (0, b))]
    for _ in codes:
        in_specs.append(pl.BlockSpec((tokens + scale_rows, bc), lambda b, s: (0, b)))
    return pl.pallas_call(
        body,
        out_shape=jax.ShapeDtypeStruct((2, n * tokens, cols), jnp.bfloat16),
        grid_spec=pltpu.PrefetchScalarGridSpec(
            num_scalar_prefetch=1,
            grid=(cols // bc,),
            in_specs=in_specs,
            out_specs=pl.BlockSpec((2, n * tokens, bc), lambda b, s: (0, 0, b)),
        ),
        compiler_params=pltpu.CompilerParams(dimension_semantics=("arbitrary",)),
        cost_estimate=pl.CostEstimate(
            flops=8 * n * tokens * cols, transcendentals=n * tokens * cols, bytes_accessed=8 * n * tokens * cols
        ),
        name="split",
    )(place, squares, rotated, *codes)


def pair_plan(width, length, block):
    rows = []
    for place in range(width):
        lo, count, kept, plan, step = 0, length // block, [], [], 1
        while step < width:
            count //= 2
            upper = place // step % 2
            start = lo + (1 - upper) * count
            plan += [start] + [start - k for k in kept]
            lo += upper * count
            kept.append(lo)
            step *= 2
        rows.append(plan + [lo] + [lo - k for k in kept])
    return rows


def pair_step(rows, scaled, received, plan, first, shift, length, block, mode, other=None, rank_count=None):
    depth = rows.shape[1]
    group = scaled.shape[1]
    nb = length // block
    n = len(received)

    def body(plan_ref, row_ref, scaled_ref, *refs):
        both = scaled_ref[...].reshape(2 * group, depth)
        product = lax.dot_general(
            row_ref[...], both, (((1,), (1,)), ((), ())), preferred_element_type=jnp.float32
        )
        total = product[:, :group] + product[:, group:]
        for i in range(n):
            total = total + decode(refs[i])
        out_ref = refs[-1]
        if mode == "code":
            encode(total, out_ref)
        elif mode == "plain":
            out_ref[...] = total
        else:
            joined = total * refs[n][...]
            out_ref[...] = jnp.sum(joined.reshape(block // rank_count, rank_count, group), axis=1)

    in_specs = [
        pl.BlockSpec((block, depth), lambda b, s: (s[first] + shift + b, 0)),
        pl.BlockSpec((2, group, depth), lambda b, s: (0, 0, 0), pipeline_mode=pl.Buffered(1)),
    ]
    for i in range(n):
        in_specs.append(pl.BlockSpec((block + scale_rows, group), lambda b, s, i=i: (s[first + 1 + i] + b, 0)))
    operands = [rows, scaled, *received]
    if mode == "code":
        out_shape = jax.ShapeDtypeStruct((nb * (block + scale_rows), group), jnp.bfloat16)
        out_spec = pl.BlockSpec((block + scale_rows, group), lambda b, s: (b, 0))
    elif mode == "plain":
        out_shape = jax.ShapeDtypeStruct((length, group), jnp.float32)
        out_spec = pl.BlockSpec((block, group), lambda b, s: (b, 0))
    else:
        in_specs.append(pl.BlockSpec((block, group), lambda b, s: (b, 0)))
        operands.append(other)
        out_shape = jax.ShapeDtypeStruct((length // rank_count, group), jnp.float32)
        out_spec = pl.BlockSpec((block // rank_count, group), lambda b, s: (b, 0))
    return pl.pallas_call(
        body,
        out_shape=out_shape,
        grid_spec=pltpu.PrefetchScalarGridSpec(
            num_scalar_prefetch=1, grid=(nb,), in_specs=in_specs, out_specs=out_spec
        ),
        compiler_params=pltpu.CompilerParams(dimension_semantics=("arbitrary",)),
        cost_estimate=pl.CostEstimate(
            flops=4 * length * depth * group,
            transcendentals=2 * length * group,
            bytes_accessed=length * depth * 2 + 2 * group * depth * 2,
        ),
        name="pair_" + mode,
    )(plan, *operands)


def reduce_pairs(rows, scaled, plan, offset, first_row, length, block, width, others=None, rank_count=None):
    received = []
    step, first, shift = 1, offset, first_row // block
    while step < width:
        length //= 2
        code = pair_step(rows, scaled, received, plan, first, shift, length, block, "code")
        first += 1 + len(received)
        received = received + [lax.ppermute(code, "width", [(i, i ^ step) for i in range(width)])]
        step *= 2
    mode = "plain" if others is None else "joined"
    return pair_step(rows, scaled, received, plan, first, shift, length, block, mode, others, rank_count)


def after(x, *earlier):
    return lax.optimization_barrier((x, *earlier))[0]


def gather_rotate(own, basis, plan, width, part_count, gate):
    even, odd = swap_pairs(width)
    count = 2 * width - 2
    send = own if gate is None else after(own, gate)
    rows = own.shape[0] // part_count
    parts = [send[i * rows : (i + 1) * rows] for i in range(part_count)] if part_count > 1 else [send]
    send_even, send_odd = parts, parts
    early, late, late_gate = [[own]], [], None
    for distance in range(1, width):
        got_even, got_odd = [], []
        for i in range(part_count):
            got_even.append(lax.ppermute(send_even[i], "width", even))
            if distance < width - 1:
                got_odd.append(lax.ppermute(send_odd[i], "width", odd))
        buffers = early if distance <= width // 2 - 1 else late
        buffers.append(got_even)
        if distance < width - 1:
            buffers.append(got_odd)
            late_gate = got_odd[-1]
        send_even, send_odd = got_odd, got_even
    acc = rotate_step(None, 0, early, basis, plan, count, not late)
    if late:
        acc = rotate_step(acc, len(early), late, basis, plan, count, True)
    return acc, late_gate


def sum_over(x, axis):
    count = lax.axis_size(axis)
    total = x
    for by in range(1, count):
        total = total + lax.ppermute(x, axis, shift_pairs(count, by))
    return total


def scaled_group(rotated, squares, code, place, total_tokens):
    count = lax.axis_size("query")
    squares = sum_over(squares, "query")
    if count > 1:
        code = after(code, squares)
    codes = [lax.ppermute(code, "query", shift_pairs(count, by)) for by in range(1, count)]
    squares = sum_over(squares, "token")
    return split_scaled(rotated, codes, squares, place, total_tokens)


def on_device(layer_inputs, out_grads, basis_in, basis_out, query_in, query_out):
    width = lax.axis_size("width")
    place = lax.axis_index("width")
    total_tokens = layer_inputs.shape[0] * lax.axis_size("token") * lax.axis_size("query")
    queries, rank_count, width_cols = query_in.shape
    rows_in = query_in.reshape(-1, width_cols)
    rows_out = query_out.reshape(-1, width_cols)
    length = rows_in.shape[0] // chunks
    block = min(row_block, length // width)

    depth = layer_inputs.shape[1]
    rotate_rows = rotate_plan(width, depth // min(basis_block, depth))
    pair_rows = pair_plan(width, length, block)
    offset = len(rotate_rows[0])
    table = jnp.asarray([a + b for a, b in zip(rotate_rows, pair_rows)], jnp.int32)
    plan = lax.dynamic_index_in_dim(table, place, keepdims=False)
    query_place = lax.axis_index("query").astype(jnp.int32)[None]

    got_in, gate = gather_rotate(layer_inputs, basis_in, plan, width, parts_in, None)
    got_out, _ = gather_rotate(out_grads, basis_out, plan, width, parts_out, gate)
    scaled_in = scaled_group(*got_in, query_place, total_tokens)
    scaled_out = scaled_group(*got_out, query_place, total_tokens)

    pairs_in = [
        reduce_pairs(rows_in, scaled_in, plan, offset, c * length, length, block, width) for c in range(chunks)
    ]
    scores = jnp.stack(
        [
            reduce_pairs(
                rows_out, scaled_out, plan, offset, c * length, length, block, width, pairs_in[c], rank_count
            )
            for c in range(chunks)
        ]
    )
    step = width // 2
    while step:
        got = lax.ppermute(scores, "width", [(i, i ^ step) for i in range(width)])
        upper = (place // step) % 2
        scores = jnp.where(
            upper == 0, jnp.concatenate([scores, got], axis=1), jnp.concatenate([got, scores], axis=1)
        )
        step //= 2
    return scores.reshape(queries, scores.shape[-1])


def solution(mesh):
    return jax.shard_map(
        on_device,
        mesh=mesh,
        in_specs=(
            P(("token", "query"), "width"),
            P(("token", "query"), "width"),
            P(None, "width"),
            P(None, "width"),
            P("query", None, "width"),
            P("query", None, "width"),
        ),
        out_specs=P("query", "token"),
        check_vma=False,
    )
```

```python
import jax
import jax.numpy as jnp
from jax import lax
from jax.experimental import pallas as pl
from jax.experimental.pallas import tpu as pltpu
from jax.sharding import PartitionSpec as P


damping = 0.1
reach = 172.0
floor = 1e-30
scale_rows = 16
row_block = 512
basis_block = 1024
basis_streams = 2
split_block = 512
chunks = 2


def swap_pairs(count):
    even = [(i, i ^ 1) for i in range(count)]
    odd = [(0, 0), (count - 1, count - 1)] + [(i, i + 1 if i % 2 else i - 1) for i in range(1, count - 1)]
    return even, odd


def shift_pairs(count, by):
    return [(i, (i + by) % count) for i in range(count)]


def line_sources(width, place):
    got = []
    for distance in range(1, width):
        right, left = place + distance, place - distance
        pair = (right, left) if place % 2 == 0 else (left, right)
        got += [pair[0]] if distance == width - 1 else list(pair)
    return [source if 0 <= source < width else None for source in got]


def rotate_plan(width, nk):
    rows = []
    for place in range(width):
        sources = [place] + line_sources(width, place)
        blocks, hold = [], 0
        for source in sources:
            for k in range(nk):
                hold = hold if source is None else source * nk + k
                blocks.append(hold)
        rows.append(blocks + [int(source is not None) for source in sources])
    return rows


def rotate_step(acc, first, buffers, basis, plan, count, last):
    tokens, depth = buffers[0].shape
    cols = basis.shape[1]
    bk = min(basis_block, depth)
    nk = depth // bk
    n = len(buffers)
    has_acc = acc is not None

    def body(plan_ref, *refs):
        chunk_refs, refs = refs[:n], refs[n:]
        basis_refs = refs[:basis_streams]
        acc_ref = refs[basis_streams] if has_acc else None
        out_refs = refs[basis_streams + has_acc :]
        out_ref = out_refs[0]
        c, k = pl.program_id(0), pl.program_id(1)

        @pl.when((c == 0) & (k == 0))
        def _():
            if has_acc:
                out_ref[...] = acc_ref[...]
            else:
                out_ref[...] = jnp.zeros_like(out_ref)

        for i in range(n):
            @pl.when((c == i) & (plan_ref[count * nk + first + i] > 0))
            def _():
                chunk = chunk_refs[i][...]
                piece = bk // basis_streams
                total = out_ref[...]
                for j in range(basis_streams):
                    total += jnp.dot(
                        chunk[:, j * piece : (j + 1) * piece], basis_refs[j][...], preferred_element_type=jnp.float32
                    )
                out_ref[...] = total

        if last:
            @pl.when((c == n - 1) & (k == nk - 1))
            def _():
                total = out_ref[...]
                out_refs[1][...] = jnp.sum(total * total, axis=0, keepdims=True)
                encode(total, out_refs[2])

    whole = pl.BlockSpec((tokens, cols), lambda c, k, s: (0, 0))
    in_specs = []
    for i in range(n):
        in_specs.append(
            pl.BlockSpec(
                (tokens, bk), lambda c, k, s, i=i: (0, jnp.where(c == i, k, jnp.where(c < i, 0, nk - 1)))
            )
        )
    for j in range(basis_streams):
        in_specs.append(
            pl.BlockSpec(
                (bk // basis_streams, cols),
                lambda c, k, s, j=j: (s[(first + c) * nk + k] * basis_streams + j, 0),
            )
        )
    operands = [*buffers, *[basis] * basis_streams]
    if has_acc:
        in_specs.append(whole)
        operands.append(acc)
    out_shape = [jax.ShapeDtypeStruct((tokens, cols), jnp.float32)]
    out_specs = [whole]
    if last:
        out_shape.append(jax.ShapeDtypeStruct((1, cols), jnp.float32))
        out_specs.append(pl.BlockSpec((1, cols), lambda c, k, s: (0, 0)))
        out_shape.append(jax.ShapeDtypeStruct((tokens + scale_rows, cols), jnp.bfloat16))
        out_specs.append(pl.BlockSpec((tokens + scale_rows, cols), lambda c, k, s: (0, 0)))
    out = pl.pallas_call(
        body,
        out_shape=out_shape,
        grid_spec=pltpu.PrefetchScalarGridSpec(
            num_scalar_prefetch=1, grid=(n, nk), in_specs=in_specs, out_specs=out_specs
        ),
        compiler_params=pltpu.CompilerParams(dimension_semantics=("arbitrary", "arbitrary")),
        cost_estimate=pl.CostEstimate(
            flops=4 * tokens * depth * cols, transcendentals=0, bytes_accessed=2 * depth * cols * 2 + tokens * cols * 8
        ),
        name="rotate",
    )(plan, *operands)
    return out if last else out[0]


def encode(value, out_ref):
    count = value.shape[0]
    top = jnp.max(jnp.abs(value), axis=0, keepdims=True)
    top = jnp.maximum(top * (1 + 2.0**-7), floor).astype(jnp.bfloat16)
    size = jnp.exp(jnp.abs(value) * (reach / top.astype(jnp.float32)) - reach / 2)
    out_ref[:count, :] = jnp.where(value < 0, -size, size).astype(jnp.bfloat16)
    out_ref[count:, :] = jnp.broadcast_to(top, (scale_rows, value.shape[1]))


def decode(ref):
    count = ref.shape[0] - scale_rows
    code = ref[:count, :].astype(jnp.float32)
    top = ref[count : count + 1, :].astype(jnp.float32)
    size = (jnp.log(jnp.abs(code)) + reach / 2) * (top * (1.0 / reach))
    return jnp.where(code < 0, -size, size)


def split_scaled(rotated, codes, squares, place, total_tokens):
    n = 1 + len(codes)
    tokens, cols = rotated.shape
    bc = min(split_block, cols)

    def body(place_ref, squares_ref, *refs):
        out_ref = refs[-1]
        gain = 1.0 / (squares_ref[...] / total_tokens + damping)
        for by in range(n):
            scaled = (refs[0][...] if by == 0 else decode(refs[by])) * gain
            head = scaled.astype(jnp.bfloat16)
            slot = lax.rem(place_ref[0] + (n - by), n) * tokens
            rows = pl.ds(pl.multiple_of(slot, tokens), tokens)
            out_ref[0, rows, :] = head
            out_ref[1, rows, :] = (scaled - head.astype(jnp.float32)).astype(jnp.bfloat16)

    in_specs = [pl.BlockSpec((1, bc), lambda b, s: (0, b)), pl.BlockSpec((tokens, bc), lambda b, s: (0, b))]
    for _ in codes:
        in_specs.append(pl.BlockSpec((tokens + scale_rows, bc), lambda b, s: (0, b)))
    return pl.pallas_call(
        body,
        out_shape=jax.ShapeDtypeStruct((2, n * tokens, cols), jnp.bfloat16),
        grid_spec=pltpu.PrefetchScalarGridSpec(
            num_scalar_prefetch=1,
            grid=(cols // bc,),
            in_specs=in_specs,
            out_specs=pl.BlockSpec((2, n * tokens, bc), lambda b, s: (0, 0, b)),
        ),
        compiler_params=pltpu.CompilerParams(dimension_semantics=("arbitrary",)),
        cost_estimate=pl.CostEstimate(
            flops=8 * n * tokens * cols, transcendentals=n * tokens * cols, bytes_accessed=8 * n * tokens * cols
        ),
        name="split",
    )(place, squares, rotated, *codes)


def pair_plan(width, length, block):
    rows = []
    for place in range(width):
        lo, count, kept, plan, step = 0, length // block, [], [], 1
        while step < width:
            count //= 2
            upper = place // step % 2
            start = lo + (1 - upper) * count
            plan += [start] + [start - k for k in kept]
            lo += upper * count
            kept.append(lo)
            step *= 2
        rows.append(plan + [lo] + [lo - k for k in kept])
    return rows


def pair_step(rows, scaled, received, plan, first, shift, length, block, mode, other=None, rank_count=None):
    depth = rows.shape[1]
    group = scaled.shape[1]
    nb = length // block
    n = len(received)

    def body(plan_ref, row_ref, scaled_ref, *refs):
        both = scaled_ref[...].reshape(2 * group, depth)
        product = lax.dot_general(
            row_ref[...], both, (((1,), (1,)), ((), ())), preferred_element_type=jnp.float32
        )
        total = product[:, :group] + product[:, group:]
        for i in range(n):
            total = total + decode(refs[i])
        out_ref = refs[-1]
        if mode == "code":
            encode(total, out_ref)
        elif mode == "plain":
            out_ref[...] = total
        else:
            joined = total * refs[n][...]
            out_ref[...] = jnp.sum(joined.reshape(block // rank_count, rank_count, group), axis=1)

    in_specs = [
        pl.BlockSpec((block, depth), lambda b, s: (s[first] + shift + b, 0)),
        pl.BlockSpec((2, group, depth), lambda b, s: (0, 0, 0), pipeline_mode=pl.Buffered(1)),
    ]
    for i in range(n):
        in_specs.append(pl.BlockSpec((block + scale_rows, group), lambda b, s, i=i: (s[first + 1 + i] + b, 0)))
    operands = [rows, scaled, *received]
    if mode == "code":
        out_shape = jax.ShapeDtypeStruct((nb * (block + scale_rows), group), jnp.bfloat16)
        out_spec = pl.BlockSpec((block + scale_rows, group), lambda b, s: (b, 0))
    elif mode == "plain":
        out_shape = jax.ShapeDtypeStruct((length, group), jnp.float32)
        out_spec = pl.BlockSpec((block, group), lambda b, s: (b, 0))
    else:
        in_specs.append(pl.BlockSpec((block, group), lambda b, s: (b, 0)))
        operands.append(other)
        out_shape = jax.ShapeDtypeStruct((length // rank_count, group), jnp.float32)
        out_spec = pl.BlockSpec((block // rank_count, group), lambda b, s: (b, 0))
    return pl.pallas_call(
        body,
        out_shape=out_shape,
        grid_spec=pltpu.PrefetchScalarGridSpec(
            num_scalar_prefetch=1, grid=(nb,), in_specs=in_specs, out_specs=out_spec
        ),
        compiler_params=pltpu.CompilerParams(dimension_semantics=("arbitrary",)),
        cost_estimate=pl.CostEstimate(
            flops=4 * length * depth * group,
            transcendentals=2 * length * group,
            bytes_accessed=length * depth * 2 + 2 * group * depth * 2,
        ),
    )(plan, *operands)


def reduce_pairs(c, rows, scaled, plan, offset, length, block, width, others=None, rank_count=None):
    received = []
    step, first, shift = 1, offset, c * (length // block)
    while step < width:
        length //= 2
        code = pair_step(rows, scaled, received, plan, first, shift, length, block, "code")
        first += 1 + len(received)
        pairs = [(i, i ^ step) for i in range(width)]
        received = received + [lax.ppermute(code, "width", pairs)]
        step *= 2
    mode = "plain" if others is None else "joined"
    return pair_step(rows, scaled, received, plan, first, shift, length, block, mode, others, rank_count)


def gather_rotate(own, basis, plan, width):
    even, odd = swap_pairs(width)
    count = 2 * width - 2
    send_even = send_odd = own
    acc = rotate_step(None, 0, [own], basis, plan, count, width == 1)
    for distance in range(1, width):
        last = distance == width - 1
        got = [lax.ppermute(send_even, "width", even)]
        if not last:
            got.append(lax.ppermute(send_odd, "width", odd))
            send_even, send_odd = got[1], got[0]
        acc = rotate_step(acc, 2 * distance - 1, got, basis, plan, count, last)
    return acc


def sum_over(x, axis):
    count = lax.axis_size(axis)
    total = x
    for by in range(1, count):
        total = total + lax.ppermute(x, axis, shift_pairs(count, by))
    return total


def scaled_group(rotated, squares, code, place, total_tokens):
    count = lax.axis_size("query")
    codes = [lax.ppermute(code, "query", shift_pairs(count, by)) for by in range(1, count)]
    squares = sum_over(squares, "query")
    squares = sum_over(squares, "token")
    return split_scaled(rotated, codes, squares, place, total_tokens)


def compute(layer_inputs, out_grads, basis_in, basis_out, query_in, query_out):
    width = lax.axis_size("width")
    place = lax.axis_index("width")
    total_tokens = layer_inputs.shape[0] * lax.axis_size("token") * lax.axis_size("query")
    queries, rank_count, width_cols = query_in.shape
    rows_in = query_in.reshape(-1, width_cols)
    rows_out = query_out.reshape(-1, width_cols)
    length = rows_in.shape[0] // chunks
    block = min(row_block, length // width)

    depth = layer_inputs.shape[1]
    rotate_rows = rotate_plan(width, depth // min(basis_block, depth))
    pair_rows = pair_plan(width, length, block)
    offset = len(rotate_rows[0])
    table = jnp.asarray([a + b for a, b in zip(rotate_rows, pair_rows)], jnp.int32)
    plan = lax.dynamic_index_in_dim(table, place, keepdims=False)
    query_place = lax.axis_index("query").astype(jnp.int32)[None]

    got_in = gather_rotate(layer_inputs, basis_in, plan, width)
    got_out = gather_rotate(out_grads, basis_out, plan, width)
    scaled_in = scaled_group(*got_in, query_place, total_tokens)
    scaled_out = scaled_group(*got_out, query_place, total_tokens)

    pairs_in = [reduce_pairs(c, rows_in, scaled_in, plan, offset, length, block, width) for c in range(chunks)]
    scores = jnp.stack(
        [
            reduce_pairs(c, rows_out, scaled_out, plan, offset, length, block, width, pairs_in[c], rank_count)
            for c in range(chunks)
        ]
    )
    step = width // 2
    while step:
        got = lax.ppermute(scores, "width", [(i, i ^ step) for i in range(width)])
        upper = (place // step) % 2
        scores = jnp.where(
            upper == 0, jnp.concatenate([scores, got], axis=1), jnp.concatenate([got, scores], axis=1)
        )
        step //= 2
    return scores.reshape(queries, scores.shape[-1])


def solution(mesh):
    return jax.shard_map(
        compute,
        mesh=mesh,
        in_specs=(
            P(("token", "query"), "width"),
            P(("token", "query"), "width"),
            P(None, "width"),
            P(None, "width"),
            P("query", None, "width"),
            P("query", None, "width"),
        ),
        out_specs=P("query", "token"),
        check_vma=False,
    )
```

```python
import jax
import jax.numpy as jnp
from jax import lax
from jax.experimental import pallas as pl
from jax.experimental.pallas import tpu as pltpu
from jax.sharding import PartitionSpec as P


damping = 0.1
reach = 172.0
floor = 1e-30
scale_rows = 16
basis_block = 1024
basis_streams = 2
split_block = 512
chunks = 4
groups_in = ((0, 1), (2, 3))
groups_out = ((0, 1), (2,), (3,))


def swap_pairs(count):
    even = [(i, i ^ 1) for i in range(count)]
    odd = [(0, 0), (count - 1, count - 1)] + [(i, i + 1 if i % 2 else i - 1) for i in range(1, count - 1)]
    return even, odd


def shift_pairs(count, by):
    return [(i, (i + by) % count) for i in range(count)]


def line_sources(width, place):
    got = []
    for distance in range(1, width):
        right, left = place + distance, place - distance
        pair = (right, left) if place % 2 == 0 else (left, right)
        got += [pair[0]] if distance == width - 1 else list(pair)
    return [source if 0 <= source < width else None for source in got]


def rotate_plan(width, nk):
    rows = []
    for place in range(width):
        sources = [place] + line_sources(width, place)
        blocks, hold = [], 0
        for source in sources:
            for k in range(nk):
                hold = hold if source is None else source * nk + k
                blocks.append(hold)
        rows.append(blocks + [int(source is not None) for source in sources])
    return rows


def rotate_step(acc, first, buffers, basis, plan, count, last):
    tokens, depth = buffers[0].shape
    cols = basis.shape[1]
    bk = min(basis_block, depth)
    nk = depth // bk
    n = len(buffers)
    has_acc = acc is not None

    def body(plan_ref, *refs):
        chunk_refs, refs = refs[:n], refs[n:]
        if n > 1:
            picked_ref, refs = refs[-1], refs[:-1]
        basis_refs = refs[:basis_streams]
        acc_ref = refs[basis_streams] if has_acc else None
        out_refs = refs[basis_streams + has_acc :]
        out_ref = out_refs[0]
        c, k = pl.program_id(0), pl.program_id(1)

        @pl.when((c == 0) & (k == 0))
        def _():
            if has_acc:
                out_ref[...] = acc_ref[...]
            else:
                out_ref[...] = jnp.zeros_like(out_ref)

        if n > 1:
            for i in range(n):
                @pl.when(c == i)
                def _():
                    picked_ref[...] = chunk_refs[i][...]

        @pl.when(plan_ref[count * nk + first + c] > 0)
        def _():
            chunk_ref = picked_ref if n > 1 else chunk_refs[0]
            piece = bk // basis_streams
            total = out_ref[...]
            for j in range(basis_streams):
                total += jnp.dot(
                    chunk_ref[:, j * piece : (j + 1) * piece], basis_refs[j][...], preferred_element_type=jnp.float32
                )
            out_ref[...] = total

        if last:
            @pl.when((c == n - 1) & (k == nk - 1))
            def _():
                total = out_ref[...]
                out_refs[1][...] = jnp.sum(total * total, axis=0, keepdims=True)
                encode(total, out_refs[2])

    whole = pl.BlockSpec((tokens, cols), lambda c, k, s: (0, 0))
    in_specs = []
    for i in range(n):
        in_specs.append(
            pl.BlockSpec(
                (tokens, bk), lambda c, k, s, i=i: (0, jnp.where(c == i, k, jnp.where(c < i, 0, nk - 1)))
            )
        )
    for j in range(basis_streams):
        in_specs.append(
            pl.BlockSpec(
                (bk // basis_streams, cols),
                lambda c, k, s, j=j: (s[(first + c) * nk + k] * basis_streams + j, 0),
            )
        )
    operands = [*buffers, *[basis] * basis_streams]
    if has_acc:
        in_specs.append(whole)
        operands.append(acc)
    out_shape = [jax.ShapeDtypeStruct((tokens, cols), jnp.float32)]
    out_specs = [whole]
    if last:
        out_shape.append(jax.ShapeDtypeStruct((1, cols), jnp.float32))
        out_specs.append(pl.BlockSpec((1, cols), lambda c, k, s: (0, 0)))
        out_shape.append(jax.ShapeDtypeStruct((tokens + scale_rows, cols), jnp.bfloat16))
        out_specs.append(pl.BlockSpec((tokens + scale_rows, cols), lambda c, k, s: (0, 0)))
    out = pl.pallas_call(
        body,
        out_shape=out_shape,
        grid_spec=pltpu.PrefetchScalarGridSpec(
            num_scalar_prefetch=1,
            grid=(n, nk),
            in_specs=in_specs,
            out_specs=out_specs,
            scratch_shapes=[pltpu.VMEM((tokens, bk), jnp.bfloat16)] if n > 1 else [],
        ),
        compiler_params=pltpu.CompilerParams(dimension_semantics=("arbitrary", "arbitrary")),
        cost_estimate=pl.CostEstimate(
            flops=4 * tokens * depth * cols, transcendentals=0, bytes_accessed=2 * depth * cols * 2 + tokens * cols * 8
        ),
        name="rotate",
    )(plan, *operands)
    return out if last else out[0]


def encode(value, out_ref):
    count = value.shape[0]
    top = jnp.max(jnp.abs(value), axis=0, keepdims=True)
    top = jnp.maximum(top * (1 + 2.0**-7), floor).astype(jnp.bfloat16)
    size = jnp.exp(jnp.abs(value) * (reach / top.astype(jnp.float32)) - reach / 2)
    out_ref[:count, :] = jnp.where(value < 0, -size, size).astype(jnp.bfloat16)
    out_ref[count:, :] = jnp.broadcast_to(top, (scale_rows, value.shape[1]))


def decode(ref):
    count = ref.shape[0] - scale_rows
    code = ref[:count, :].astype(jnp.float32)
    top = ref[count : count + 1, :].astype(jnp.float32)
    size = (jnp.log(jnp.abs(code)) + reach / 2) * (top * (1.0 / reach))
    return jnp.where(code < 0, -size, size)


def split_scaled(rotated, codes, squares, place, total_tokens):
    n = 1 + len(codes)
    tokens, cols = rotated.shape
    bc = min(split_block, cols)

    def body(place_ref, *refs):
        out_ref = refs[-1]
        squares_total = refs[0][...]
        for ref in refs[1 : len(squares)]:
            squares_total += ref[...]
        refs = refs[len(squares) :]
        gain = 1.0 / (squares_total / total_tokens + damping)
        for by in range(n):
            scaled = (refs[0][...] if by == 0 else decode(refs[by])) * gain
            head = scaled.astype(jnp.bfloat16)
            slot = lax.rem(place_ref[0] + (n - by), n) * tokens
            rows = pl.ds(pl.multiple_of(slot, tokens), tokens)
            out_ref[0, rows, :] = head
            out_ref[1, rows, :] = (scaled - head.astype(jnp.float32)).astype(jnp.bfloat16)

    in_specs = [pl.BlockSpec((1, bc), lambda b, s: (0, b)) for _ in squares]
    in_specs.append(pl.BlockSpec((tokens, bc), lambda b, s: (0, b)))
    for _ in codes:
        in_specs.append(pl.BlockSpec((tokens + scale_rows, bc), lambda b, s: (0, b)))
    return pl.pallas_call(
        body,
        out_shape=jax.ShapeDtypeStruct((2, n * tokens, cols), jnp.bfloat16),
        grid_spec=pltpu.PrefetchScalarGridSpec(
            num_scalar_prefetch=1,
            grid=(cols // bc,),
            in_specs=in_specs,
            out_specs=pl.BlockSpec((2, n * tokens, bc), lambda b, s: (0, 0, b)),
        ),
        compiler_params=pltpu.CompilerParams(dimension_semantics=("arbitrary",)),
        cost_estimate=pl.CostEstimate(
            flops=8 * n * tokens * cols, transcendentals=n * tokens * cols, bytes_accessed=8 * n * tokens * cols
        ),
        name="split",
    )(place, *squares, rotated, *codes)


def mirror(place, width):
    part, step = 0, 1
    while step < width:
        part = 2 * part + place // step % 2
        step *= 2
    return part


def pair_plan(width, size):
    rows = []
    for place in range(width):
        lo, count, kept, steps, step = 0, width, [], [], 1
        while step <= width:
            count //= 2
            upper = place // step % 2
            start_at = lo + (1 - upper) * count
            if step == width:
                start_at, count = lo, 1
            steps.append(
                [
                    [c * width + start_at + i] + [c * many + start_at + i - base for base, many in kept]
                    for c in range(size)
                    for i in range(count)
                ]
            )
            lo += upper * count if step < width else 0
            kept.append((lo, count))
            step *= 2
        rows.append(steps)
    return rows


def pair_step(rows, scaled, received, plan, first, shift, nb, block, mode, other=None, rank_count=None):
    depth = rows.shape[1]
    group = scaled.shape[1]
    n = len(received)
    length = nb * block

    def body(plan_ref, row_ref, scaled_ref, *refs):
        both = scaled_ref[...].reshape(2 * group, depth)
        product = lax.dot_general(
            row_ref[...], both, (((1,), (1,)), ((), ())), preferred_element_type=jnp.float32
        )
        total = product[:, :group] + product[:, group:]
        for i in range(n):
            total = total + decode(refs[i])
        out_ref = refs[-1]
        if mode == "code":
            encode(total, out_ref)
        elif mode == "plain":
            out_ref[...] = total
        else:
            joined = total * refs[n][...]
            out_ref[0] = jnp.sum(joined.reshape(block // rank_count, rank_count, group), axis=1)

    def place_of(column):
        return lambda b, s: (s[first + b * (n + 1) + column] + (shift if column == 0 else 0), 0)

    in_specs = [
        pl.BlockSpec((block, depth), place_of(0)),
        pl.BlockSpec((2, group, depth), lambda b, s: (0, 0, 0), pipeline_mode=pl.Buffered(1)),
    ]
    for i in range(n):
        in_specs.append(pl.BlockSpec((block + scale_rows, group), place_of(1 + i)))
    operands = [rows, scaled, *received]
    if mode == "code":
        out_shape = jax.ShapeDtypeStruct((nb * (block + scale_rows), group), jnp.bfloat16)
        out_spec = pl.BlockSpec((block + scale_rows, group), lambda b, s: (b, 0))
    elif mode == "plain":
        out_shape = jax.ShapeDtypeStruct((length, group), jnp.float32)
        out_spec = pl.BlockSpec((block, group), lambda b, s: (b, 0))
    else:
        other, at = other
        in_specs.append(pl.BlockSpec((block, group), lambda b, s: (at + b, 0)))
        operands.append(other)
        out_shape = jax.ShapeDtypeStruct((nb, block // rank_count, group), jnp.float32)
        out_spec = pl.BlockSpec((1, block // rank_count, group), lambda b, s: (b, 0, 0))
    return pl.pallas_call(
        body,
        out_shape=out_shape,
        grid_spec=pltpu.PrefetchScalarGridSpec(
            num_scalar_prefetch=1, grid=(nb,), in_specs=in_specs, out_specs=out_spec
        ),
        compiler_params=pltpu.CompilerParams(dimension_semantics=("arbitrary",)),
        cost_estimate=pl.CostEstimate(
            flops=4 * length * depth * group,
            transcendentals=2 * length * group,
            bytes_accessed=length * depth * 2 + 2 * group * depth * 2,
        ),
    )(plan, *operands)


def reduce_pairs(members, rows, scaled, plan, firsts, block, width, other=None, rank_count=None):
    received = []
    step, nb, shift = 1, len(members) * width, members[0] * width
    while step < width:
        nb //= 2
        code = pair_step(rows, scaled, received, plan, firsts[len(received)], shift, nb, block, "code")
        pairs = [(i, i ^ step) for i in range(width)]
        received = received + [in_hbm(lax.ppermute(code, "width", pairs))]
        step *= 2
    mode = "plain" if other is None else "joined"
    return pair_step(
        rows, scaled, received, plan, firsts[len(received)], shift, nb, block, mode, other, rank_count
    )


def assemble(batches, plan, first):
    width = len(batches[0])
    arrays = [array for batch in batches for array in batch]
    total = sum(batch[0].shape[0] for batch in batches)

    def body(plan_ref, *refs):
        out_ref = refs[-1]
        base = 0
        for b, batch in enumerate(batches):
            size = batch[0].shape[0]
            for x in range(width):
                for c in range(size):
                    out_ref[base + c, pl.ds(plan_ref[first + x], 1)] = refs[b * width + x][pl.ds(c, 1)]
            base += size

    return pl.pallas_call(
        body,
        out_shape=jax.ShapeDtypeStruct((total, width) + arrays[0].shape[1:], jnp.float32),
        in_specs=[pl.BlockSpec(memory_space=pltpu.SMEM)] + [pl.BlockSpec(memory_space=pltpu.VMEM)] * len(arrays),
        out_specs=pl.BlockSpec(memory_space=pltpu.VMEM),
        name="assemble",
    )(plan, *arrays)


def in_hbm(x):
    return pltpu.with_memory_space_constraint(x, pltpu.HBM)


def gather_rotate(own, basis, plan, width):
    even, odd = swap_pairs(width)
    count = 2 * width - 2
    send_even = send_odd = own
    acc = rotate_step(None, 0, [own], basis, plan, count, width == 1)
    for distance in range(1, width):
        last = distance == width - 1
        got = [lax.ppermute(send_even, "width", even)]
        if not last:
            got.append(lax.ppermute(send_odd, "width", odd))
            send_even, send_odd = got[1], got[0]
        acc = rotate_step(acc, 2 * distance - 1, [in_hbm(x) for x in got], basis, plan, count, last)
    return acc


def scaled_group(rotated, squares, code, place, total_tokens):
    query_count, token_count = lax.axis_size("query"), lax.axis_size("token")
    codes, total = [], squares
    for by in range(1, query_count):
        shifted = shift_pairs(query_count, by)
        codes.append(in_hbm(lax.ppermute(code, "query", shifted)))
        total = total + lax.ppermute(squares, "query", shifted)
    sums = [total] + [lax.ppermute(total, "token", shift_pairs(token_count, by)) for by in range(1, token_count)]
    return split_scaled(rotated, codes, sums, place, total_tokens)


def compute(layer_inputs, out_grads, basis_in, basis_out, query_in, query_out):
    width = lax.axis_size("width")
    place = lax.axis_index("width")
    total_tokens = layer_inputs.shape[0] * lax.axis_size("token") * lax.axis_size("query")
    queries, rank_count, width_cols = query_in.shape
    rows_in = query_in.reshape(-1, width_cols)
    rows_out = query_out.reshape(-1, width_cols)
    block = rows_in.shape[0] // (chunks * width)

    depth = layer_inputs.shape[1]
    table = rotate_plan(width, depth // min(basis_block, depth))
    firsts = {}
    for size in sorted({len(members) for members in groups_in + groups_out}):
        firsts[size] = []
        for step in range(len(pair_plan(width, size)[0])):
            firsts[size].append(len(table[0]))
            for at, steps in enumerate(pair_plan(width, size)):
                table[at] += [number for entry in steps[step] for number in entry]
    parts_at = len(table[0])
    for at in range(width):
        table[at] += [mirror(at ^ x, width) for x in range(width)]
    plan = lax.dynamic_index_in_dim(jnp.asarray(table, jnp.int32), place, keepdims=False)
    query_place = lax.axis_index("query").astype(jnp.int32)[None]

    got_in = gather_rotate(layer_inputs, basis_in, plan, width)
    got_out = gather_rotate(out_grads, basis_out, plan, width)
    scaled_in = scaled_group(*got_in, query_place, total_tokens)
    scaled_out = scaled_group(*got_out, query_place, total_tokens)

    found = {}
    for members in groups_in:
        pairs = reduce_pairs(members, rows_in, scaled_in, plan, firsts[len(members)], block, width)
        found.update({c: (pairs, i) for i, c in enumerate(members)})
    batches = []
    for members in groups_out:
        own = reduce_pairs(
            members, rows_out, scaled_out, plan, firsts[len(members)], block, width, found[members[0]], rank_count
        )
        batches.append(
            [own] + [lax.ppermute(own, "width", [(i, i ^ x) for i in range(width)]) for x in range(1, width)]
        )
    scores = assemble(batches, plan, parts_at)
    return scores.reshape(queries, scores.shape[-1])


def solution(mesh):
    return jax.shard_map(
        compute,
        mesh=mesh,
        in_specs=(
            P(("token", "query"), "width"),
            P(("token", "query"), "width"),
            P(None, "width"),
            P(None, "width"),
            P("query", None, "width"),
            P("query", None, "width"),
        ),
        out_specs=P("query", "token"),
        check_vma=False,
    )
```

```python
import jax
import jax.numpy as jnp
from jax import lax
from jax.experimental import pallas as pl
from jax.experimental.pallas import tpu as pltpu
from jax.sharding import PartitionSpec as P


damping = 0.1
reach = 172.0
floor = 1e-30
scale_rows = 16
basis_block = 1024
basis_streams = 2
split_block = 512
chunks = 4
groups_in = ((0, 1), (2, 3))
groups_out = ((0, 1), (2,), (3,))


def swap_pairs(count):
    even = [(i, i ^ 1) for i in range(count)]
    odd = [(0, 0), (count - 1, count - 1)] + [(i, i + 1 if i % 2 else i - 1) for i in range(1, count - 1)]
    return even, odd


def shift_pairs(count, by):
    return [(i, (i + by) % count) for i in range(count)]


def far_pairs(count):
    return [(0, count - 1), (count - 1, 0)] + [(i, i) for i in range(1, count - 1)]


def line_sources(width, place):
    got = []
    for distance in range(1, max(width - 1, 2) if width > 1 else 1):
        right, left = place + distance, place - distance
        got += [right, left] if place % 2 == 0 else [left, right]
        if distance == 1:
            if width == 2:
                got = got[:1]
            else:
                got.append(width - 1 if place == 0 else 0 if place == width - 1 else None)
    return [source if source is not None and 0 <= source < width else None for source in got]


def rotate_plan(width, nk):
    rows = []
    for place in range(width):
        sources = [place] + line_sources(width, place)
        blocks, hold = [], 0
        for source in sources:
            for k in range(nk):
                hold = hold if source is None else source * nk + k
                blocks.append(hold)
        rows.append(blocks + [int(source is not None) for source in sources])
    return rows


def rotate_step(acc, first, buffers, basis, plan, count, last):
    tokens, depth = buffers[0].shape
    cols = basis.shape[1]
    bk = min(basis_block, depth)
    nk = depth // bk
    n = len(buffers)
    has_acc = acc is not None

    def body(plan_ref, *refs):
        chunk_refs, refs = refs[:n], refs[n:]
        if n > 1:
            picked_ref, refs = refs[-1], refs[:-1]
        basis_refs = refs[:basis_streams]
        acc_ref = refs[basis_streams] if has_acc else None
        out_refs = refs[basis_streams + has_acc :]
        out_ref = out_refs[0]
        c, k = pl.program_id(0), pl.program_id(1)

        @pl.when((c == 0) & (k == 0))
        def _():
            if has_acc:
                out_ref[...] = acc_ref[...]
            else:
                out_ref[...] = jnp.zeros_like(out_ref)

        if n > 1:
            for i in range(n):
                @pl.when(c == i)
                def _():
                    picked_ref[...] = chunk_refs[i][...]

        @pl.when(plan_ref[count * nk + first + c] > 0)
        def _():
            chunk_ref = picked_ref if n > 1 else chunk_refs[0]
            piece = bk // basis_streams
            total = out_ref[...]
            for j in range(basis_streams):
                total += jnp.dot(
                    chunk_ref[:, j * piece : (j + 1) * piece], basis_refs[j][...], preferred_element_type=jnp.float32
                )
            out_ref[...] = total

        if last:
            @pl.when((c == n - 1) & (k == nk - 1))
            def _():
                total = out_ref[...]
                out_refs[1][...] = jnp.sum(total * total, axis=0, keepdims=True)
                encode(total, out_refs[2])

    whole = pl.BlockSpec((tokens, cols), lambda c, k, s: (0, 0))
    in_specs = []
    for i in range(n):
        in_specs.append(
            pl.BlockSpec(
                (tokens, bk), lambda c, k, s, i=i: (0, jnp.where(c == i, k, jnp.where(c < i, 0, nk - 1)))
            )
        )
    for j in range(basis_streams):
        in_specs.append(
            pl.BlockSpec(
                (bk // basis_streams, cols),
                lambda c, k, s, j=j: (s[(first + c) * nk + k] * basis_streams + j, 0),
            )
        )
    operands = [*buffers, *[basis] * basis_streams]
    if has_acc:
        in_specs.append(whole)
        operands.append(acc)
    out_shape = [jax.ShapeDtypeStruct((tokens, cols), jnp.float32)]
    out_specs = [whole]
    if last:
        out_shape.append(jax.ShapeDtypeStruct((1, cols), jnp.float32))
        out_specs.append(pl.BlockSpec((1, cols), lambda c, k, s: (0, 0)))
        out_shape.append(jax.ShapeDtypeStruct((tokens + scale_rows, cols), jnp.bfloat16))
        out_specs.append(pl.BlockSpec((tokens + scale_rows, cols), lambda c, k, s: (0, 0)))
    out = pl.pallas_call(
        body,
        out_shape=out_shape,
        grid_spec=pltpu.PrefetchScalarGridSpec(
            num_scalar_prefetch=1,
            grid=(n, nk),
            in_specs=in_specs,
            out_specs=out_specs,
            scratch_shapes=[pltpu.VMEM((tokens, bk), jnp.bfloat16)] if n > 1 else [],
        ),
        compiler_params=pltpu.CompilerParams(dimension_semantics=("arbitrary", "arbitrary")),
        cost_estimate=pl.CostEstimate(
            flops=4 * tokens * depth * cols, transcendentals=0, bytes_accessed=2 * depth * cols * 2 + tokens * cols * 8
        ),
        name="rotate",
    )(plan, *operands)
    return out if last else out[0]


def encode(value, out_ref):
    count = value.shape[0]
    top = jnp.max(jnp.abs(value), axis=0, keepdims=True)
    top = jnp.maximum(top * (1 + 2.0**-7), floor).astype(jnp.bfloat16)
    size = jnp.exp(jnp.abs(value) * (reach / top.astype(jnp.float32)) - reach / 2)
    out_ref[:count, :] = jnp.where(value < 0, -size, size).astype(jnp.bfloat16)
    out_ref[count:, :] = jnp.broadcast_to(top, (scale_rows, value.shape[1]))


def decode(ref):
    count = ref.shape[0] - scale_rows
    code = ref[:count, :].astype(jnp.float32)
    top = ref[count : count + 1, :].astype(jnp.float32)
    size = (jnp.log(jnp.abs(code)) + reach / 2) * (top * (1.0 / reach))
    return jnp.where(code < 0, -size, size)


def split_scaled(rotated, codes, squares, place, total_tokens):
    n = 1 + len(codes)
    tokens, cols = rotated.shape
    bc = min(split_block, cols)

    def body(place_ref, *refs):
        out_ref = refs[-1]
        squares_total = refs[0][...]
        for ref in refs[1 : len(squares)]:
            squares_total += ref[...]
        refs = refs[len(squares) :]
        gain = 1.0 / (squares_total / total_tokens + damping)
        for by in range(n):
            scaled = (refs[0][...] if by == 0 else decode(refs[by])) * gain
            head = scaled.astype(jnp.bfloat16)
            slot = lax.rem(place_ref[0] + (n - by), n) * tokens
            rows = pl.ds(pl.multiple_of(slot, tokens), tokens)
            out_ref[0, rows, :] = head
            out_ref[1, rows, :] = (scaled - head.astype(jnp.float32)).astype(jnp.bfloat16)

    in_specs = [pl.BlockSpec((1, bc), lambda b, s: (0, b)) for _ in squares]
    in_specs.append(pl.BlockSpec((tokens, bc), lambda b, s: (0, b)))
    for _ in codes:
        in_specs.append(pl.BlockSpec((tokens + scale_rows, bc), lambda b, s: (0, b)))
    return pl.pallas_call(
        body,
        out_shape=jax.ShapeDtypeStruct((2, n * tokens, cols), jnp.bfloat16),
        grid_spec=pltpu.PrefetchScalarGridSpec(
            num_scalar_prefetch=1,
            grid=(cols // bc,),
            in_specs=in_specs,
            out_specs=pl.BlockSpec((2, n * tokens, bc), lambda b, s: (0, 0, b)),
        ),
        compiler_params=pltpu.CompilerParams(dimension_semantics=("arbitrary",)),
        cost_estimate=pl.CostEstimate(
            flops=8 * n * tokens * cols, transcendentals=n * tokens * cols, bytes_accessed=8 * n * tokens * cols
        ),
        name="split",
    )(place, *squares, rotated, *codes)


def mirror(place, width):
    part, step = 0, 1
    while step < width:
        part = 2 * part + place // step % 2
        step *= 2
    return part


def pair_plan(width, size):
    rows = []
    for place in range(width):
        lo, count, kept, steps, step = 0, width, [], [], 1
        while step <= width:
            count //= 2
            upper = place // step % 2
            start_at = lo + (1 - upper) * count
            if step == width:
                start_at, count = lo, 1
            steps.append(
                [
                    [c * width + start_at + i] + [c * many + start_at + i - base for base, many in kept]
                    for c in range(size)
                    for i in range(count)
                ]
            )
            lo += upper * count if step < width else 0
            kept.append((lo, count))
            step *= 2
        rows.append(steps)
    return rows


def pair_step(rows, scaled, received, plan, first, shift, nb, block, mode, other=None, rank_count=None):
    depth = rows.shape[1]
    group = scaled.shape[1]
    n = len(received)
    length = nb * block

    def body(plan_ref, row_ref, scaled_ref, *refs):
        both = scaled_ref[...].reshape(2 * group, depth)
        product = lax.dot_general(
            row_ref[...], both, (((1,), (1,)), ((), ())), preferred_element_type=jnp.float32
        )
        total = product[:, :group] + product[:, group:]
        for i in range(n):
            total = total + decode(refs[i])
        out_ref = refs[-1]
        if mode == "code":
            encode(total, out_ref)
        elif mode == "plain":
            out_ref[...] = total
        else:
            joined = total * refs[n][...]
            out_ref[0] = jnp.sum(joined.reshape(block // rank_count, rank_count, group), axis=1)

    def place_of(column):
        return lambda b, s: (s[first + b * (n + 1) + column] + (shift if column == 0 else 0), 0)

    in_specs = [
        pl.BlockSpec((block, depth), place_of(0)),
        pl.BlockSpec((2, group, depth), lambda b, s: (0, 0, 0), pipeline_mode=pl.Buffered(1)),
    ]
    for i in range(n):
        in_specs.append(pl.BlockSpec((block + scale_rows, group), place_of(1 + i)))
    operands = [rows, scaled, *received]
    if mode == "code":
        out_shape = jax.ShapeDtypeStruct((nb * (block + scale_rows), group), jnp.bfloat16)
        out_spec = pl.BlockSpec((block + scale_rows, group), lambda b, s: (b, 0))
    elif mode == "plain":
        out_shape = jax.ShapeDtypeStruct((length, group), jnp.float32)
        out_spec = pl.BlockSpec((block, group), lambda b, s: (b, 0))
    else:
        other, at = other
        in_specs.append(pl.BlockSpec((block, group), lambda b, s: (at + b, 0)))
        operands.append(other)
        out_shape = jax.ShapeDtypeStruct((nb, block // rank_count, group), jnp.float32)
        out_spec = pl.BlockSpec((1, block // rank_count, group), lambda b, s: (b, 0, 0))
    return pl.pallas_call(
        body,
        out_shape=out_shape,
        grid_spec=pltpu.PrefetchScalarGridSpec(
            num_scalar_prefetch=1, grid=(nb,), in_specs=in_specs, out_specs=out_spec
        ),
        compiler_params=pltpu.CompilerParams(dimension_semantics=("arbitrary",)),
        cost_estimate=pl.CostEstimate(
            flops=4 * length * depth * group,
            transcendentals=2 * length * group,
            bytes_accessed=length * depth * 2 + 2 * group * depth * 2,
        ),
    )(plan, *operands)


def reduce_pairs(members, rows, scaled, plan, firsts, block, width, other=None, rank_count=None):
    received = []
    step, nb, shift = 1, len(members) * width, members[0] * width
    while step < width:
        nb //= 2
        code = pair_step(rows, scaled, received, plan, firsts[len(received)], shift, nb, block, "code")
        pairs = [(i, i ^ step) for i in range(width)]
        received = received + [in_vmem(lax.ppermute(code, "width", pairs))]
        step *= 2
    mode = "plain" if other is None else "joined"
    return pair_step(
        rows, scaled, received, plan, firsts[len(received)], shift, nb, block, mode, other, rank_count
    )


def assemble(batches, plan, first):
    width = len(batches[0])
    arrays = [array for batch in batches for array in batch]
    total = sum(batch[0].shape[0] for batch in batches)

    def body(plan_ref, *refs):
        out_ref = refs[-1]
        base = 0
        for b, batch in enumerate(batches):
            size = batch[0].shape[0]
            for x in range(width):
                for c in range(size):
                    out_ref[base + c, pl.ds(plan_ref[first + x], 1)] = refs[b * width + x][pl.ds(c, 1)]
            base += size

    return pl.pallas_call(
        body,
        out_shape=jax.ShapeDtypeStruct((total, width) + arrays[0].shape[1:], jnp.float32),
        in_specs=[pl.BlockSpec(memory_space=pltpu.SMEM)] + [pl.BlockSpec(memory_space=pltpu.VMEM)] * len(arrays),
        out_specs=pl.BlockSpec(memory_space=pltpu.VMEM),
        name="assemble",
    )(plan, *arrays)


def in_vmem(x):
    return pltpu.with_memory_space_constraint(x, pltpu.VMEM)


def gather_rotate(own, basis, plan, width):
    even, odd = swap_pairs(width)
    count = 1 + len(line_sources(width, 0))
    send_even = send_odd = own
    acc = rotate_step(None, 0, [own], basis, plan, count, width == 1)
    done = 1
    for distance in range(1, max(width - 1, 2) if width > 1 else 1):
        got = [lax.ppermute(send_even, "width", even)]
        if width > 2:
            got.append(lax.ppermute(send_odd, "width", odd))
            send_even, send_odd = got[1], got[0]
            if distance == 1:
                got.append(lax.ppermute(own, "width", far_pairs(width)))
        last = done + len(got) == count
        acc = rotate_step(acc, done, [in_vmem(x) for x in got], basis, plan, count, last)
        done += len(got)
    return acc


def scaled_group(rotated, squares, code, place, total_tokens):
    query_count, token_count = lax.axis_size("query"), lax.axis_size("token")
    codes, total = [], squares
    for by in range(1, query_count):
        shifted = shift_pairs(query_count, by)
        codes.append(in_vmem(lax.ppermute(code, "query", shifted)))
        total = total + lax.ppermute(squares, "query", shifted)
    sums = [total] + [lax.ppermute(total, "token", shift_pairs(token_count, by)) for by in range(1, token_count)]
    return split_scaled(rotated, codes, sums, place, total_tokens)


def compute(layer_inputs, out_grads, basis_in, basis_out, query_in, query_out):
    width = lax.axis_size("width")
    place = lax.axis_index("width")
    total_tokens = layer_inputs.shape[0] * lax.axis_size("token") * lax.axis_size("query")
    queries, rank_count, width_cols = query_in.shape
    rows_in = query_in.reshape(-1, width_cols)
    rows_out = query_out.reshape(-1, width_cols)
    block = rows_in.shape[0] // (chunks * width)

    depth = layer_inputs.shape[1]
    table = rotate_plan(width, depth // min(basis_block, depth))
    firsts = {}
    for size in sorted({len(members) for members in groups_in + groups_out}):
        firsts[size] = []
        for step in range(len(pair_plan(width, size)[0])):
            firsts[size].append(len(table[0]))
            for at, steps in enumerate(pair_plan(width, size)):
                table[at] += [number for entry in steps[step] for number in entry]
    parts_at = len(table[0])
    for at in range(width):
        table[at] += [mirror(at ^ x, width) for x in range(width)]
    plan = lax.dynamic_index_in_dim(jnp.asarray(table, jnp.int32), place, keepdims=False)
    query_place = lax.axis_index("query").astype(jnp.int32)[None]

    got_in = gather_rotate(layer_inputs, basis_in, plan, width)
    got_out = gather_rotate(out_grads, basis_out, plan, width)
    scaled_in = scaled_group(*got_in, query_place, total_tokens)
    scaled_out = scaled_group(*got_out, query_place, total_tokens)

    found = {}
    for members in groups_in:
        pairs = reduce_pairs(members, rows_in, scaled_in, plan, firsts[len(members)], block, width)
        found.update({c: (pairs, i) for i, c in enumerate(members)})
    batches = []
    for members in groups_out:
        own = reduce_pairs(
            members, rows_out, scaled_out, plan, firsts[len(members)], block, width, found[members[0]], rank_count
        )
        batches.append(own)
    own = jnp.concatenate(batches, axis=0)
    far = [lax.ppermute(own, "width", [(i, i ^ x) for i in range(width)]) for x in range(1, width)]
    scores = assemble([[own] + far], plan, parts_at)
    return scores.reshape(queries, scores.shape[-1])


def solution(mesh):
    return jax.shard_map(
        compute,
        mesh=mesh,
        in_specs=(
            P(("token", "query"), "width"),
            P(("token", "query"), "width"),
            P(None, "width"),
            P(None, "width"),
            P("query", None, "width"),
            P("query", None, "width"),
        ),
        out_specs=P("query", "token"),
        check_vma=False,
    )
```

```python
import jax
import jax.numpy as jnp
from jax import lax
from jax.experimental import pallas as pl
from jax.experimental.pallas import tpu as pltpu
from jax.sharding import PartitionSpec as P


damping = 0.1
reach = 172.0
floor = 1e-30
scale_rows = 16
basis_block = 1024
basis_streams = 2
split_block = 512
chunks = 2
groups_in = ((0,), (1,))
groups_out = ((0,), (1,))


def swap_pairs(count):
    even = [(i, i ^ 1) for i in range(count)]
    odd = [(0, 0), (count - 1, count - 1)] + [(i, i + 1 if i % 2 else i - 1) for i in range(1, count - 1)]
    return even, odd


def shift_pairs(count, by):
    return [(i, (i + by) % count) for i in range(count)]


def far_pairs(count):
    return [(0, count - 1), (count - 1, 0)] + [(i, i) for i in range(1, count - 1)]


def line_sources(width, place):
    got = []
    for distance in range(1, max(width - 1, 2) if width > 1 else 1):
        right, left = place + distance, place - distance
        got += [right, left] if place % 2 == 0 else [left, right]
    if width == 2:
        got = got[:1]
    elif width > 2:
        got.append(width - 1 if place == 0 else 0 if place == width - 1 else None)
    return [source if source is not None and 0 <= source < width else None for source in got]


def rotate_plan(width, nk):
    rows = []
    for place in range(width):
        sources = [place] + line_sources(width, place)
        blocks, hold = [], 0
        for source in sources:
            for k in range(nk):
                hold = hold if source is None else source * nk + k
                blocks.append(hold)
        rows.append(blocks + [int(source is not None) for source in sources])
    return rows


def rotate_step(acc, first, buffers, basis, plan, count, last):
    tokens, depth = buffers[0].shape
    cols = basis.shape[1]
    bk = min(basis_block, depth)
    nk = depth // bk
    n = len(buffers)
    has_acc = acc is not None

    def body(plan_ref, *refs):
        chunk_refs, refs = refs[:n], refs[n:]
        if n > 1:
            picked_ref, refs = refs[-1], refs[:-1]
        basis_refs = refs[:basis_streams]
        acc_ref = refs[basis_streams] if has_acc else None
        out_refs = refs[basis_streams + has_acc :]
        out_ref = out_refs[0]
        c, k = pl.program_id(0), pl.program_id(1)

        @pl.when((c == 0) & (k == 0))
        def _():
            if has_acc:
                out_ref[...] = acc_ref[...]
            else:
                out_ref[...] = jnp.zeros_like(out_ref)

        if n > 1:
            for i in range(n):
                @pl.when(c == i)
                def _():
                    picked_ref[...] = chunk_refs[i][...]

        @pl.when(plan_ref[count * nk + first + c] > 0)
        def _():
            chunk_ref = picked_ref if n > 1 else chunk_refs[0]
            piece = bk // basis_streams
            total = out_ref[...]
            for j in range(basis_streams):
                total += jnp.dot(
                    chunk_ref[:, j * piece : (j + 1) * piece], basis_refs[j][...], preferred_element_type=jnp.float32
                )
            out_ref[...] = total

        if last:
            @pl.when((c == n - 1) & (k == nk - 1))
            def _():
                total = out_ref[...]
                out_refs[1][...] = jnp.sum(total * total, axis=0, keepdims=True)
                encode(total, out_refs[2])

    whole = pl.BlockSpec((tokens, cols), lambda c, k, s: (0, 0))
    in_specs = []
    for i in range(n):
        in_specs.append(
            pl.BlockSpec(
                (tokens, bk), lambda c, k, s, i=i: (0, jnp.where(c == i, k, jnp.where(c < i, 0, nk - 1)))
            )
        )
    for j in range(basis_streams):
        in_specs.append(
            pl.BlockSpec(
                (bk // basis_streams, cols),
                lambda c, k, s, j=j: (s[(first + c) * nk + k] * basis_streams + j, 0),
            )
        )
    operands = [*buffers, *[basis] * basis_streams]
    if has_acc:
        in_specs.append(whole)
        operands.append(acc)
    out_shape = [jax.ShapeDtypeStruct((tokens, cols), jnp.float32)]
    out_specs = [whole]
    if last:
        out_shape.append(jax.ShapeDtypeStruct((1, cols), jnp.float32))
        out_specs.append(pl.BlockSpec((1, cols), lambda c, k, s: (0, 0)))
        out_shape.append(jax.ShapeDtypeStruct((tokens + scale_rows, cols), jnp.bfloat16))
        out_specs.append(pl.BlockSpec((tokens + scale_rows, cols), lambda c, k, s: (0, 0)))
    out = pl.pallas_call(
        body,
        out_shape=out_shape,
        grid_spec=pltpu.PrefetchScalarGridSpec(
            num_scalar_prefetch=1,
            grid=(n, nk),
            in_specs=in_specs,
            out_specs=out_specs,
            scratch_shapes=[pltpu.VMEM((tokens, bk), jnp.bfloat16)] if n > 1 else [],
        ),
        compiler_params=pltpu.CompilerParams(dimension_semantics=("arbitrary", "arbitrary")),
        cost_estimate=pl.CostEstimate(
            flops=4 * tokens * depth * cols, transcendentals=0, bytes_accessed=2 * depth * cols * 2 + tokens * cols * 8
        ),
        name="rotate",
    )(plan, *operands)
    return out if last else out[0]


def encode(value, out_ref):
    count = value.shape[0]
    top = jnp.max(jnp.abs(value), axis=0, keepdims=True)
    top = jnp.maximum(top * (1 + 2.0**-7), floor).astype(jnp.bfloat16)
    size = jnp.exp(jnp.abs(value) * (reach / top.astype(jnp.float32)) - reach / 2)
    out_ref[:count, :] = jnp.where(value < 0, -size, size).astype(jnp.bfloat16)
    out_ref[count:, :] = jnp.broadcast_to(top, (scale_rows, value.shape[1]))


def decode(ref):
    count = ref.shape[0] - scale_rows
    code = ref[:count, :].astype(jnp.float32)
    top = ref[count : count + 1, :].astype(jnp.float32)
    size = (jnp.log(jnp.abs(code)) + reach / 2) * (top * (1.0 / reach))
    return jnp.where(code < 0, -size, size)


def split_scaled(rotated, codes, squares, place, total_tokens):
    n = 1 + len(codes)
    tokens, cols = rotated.shape
    bc = min(split_block, cols)

    def body(place_ref, *refs):
        out_ref = refs[-1]
        squares_total = refs[0][...]
        for ref in refs[1 : len(squares)]:
            squares_total += ref[...]
        refs = refs[len(squares) :]
        gain = 1.0 / (squares_total / total_tokens + damping)
        for by in range(n):
            scaled = (refs[0][...] if by == 0 else decode(refs[by])) * gain
            head = scaled.astype(jnp.bfloat16)
            slot = lax.rem(place_ref[0] + (n - by), n) * tokens
            rows = pl.ds(pl.multiple_of(slot, tokens), tokens)
            out_ref[0, rows, :] = head
            out_ref[1, rows, :] = (scaled - head.astype(jnp.float32)).astype(jnp.bfloat16)

    in_specs = [pl.BlockSpec((1, bc), lambda b, s: (0, b)) for _ in squares]
    in_specs.append(pl.BlockSpec((tokens, bc), lambda b, s: (0, b)))
    for _ in codes:
        in_specs.append(pl.BlockSpec((tokens + scale_rows, bc), lambda b, s: (0, b)))
    return pl.pallas_call(
        body,
        out_shape=jax.ShapeDtypeStruct((2, n * tokens, cols), jnp.bfloat16),
        grid_spec=pltpu.PrefetchScalarGridSpec(
            num_scalar_prefetch=1,
            grid=(cols // bc,),
            in_specs=in_specs,
            out_specs=pl.BlockSpec((2, n * tokens, bc), lambda b, s: (0, 0, b)),
        ),
        compiler_params=pltpu.CompilerParams(dimension_semantics=("arbitrary",)),
        cost_estimate=pl.CostEstimate(
            flops=8 * n * tokens * cols, transcendentals=n * tokens * cols, bytes_accessed=8 * n * tokens * cols
        ),
        name="split",
    )(place, *squares, rotated, *codes)


def mirror(place, width):
    part, step = 0, 1
    while step < width:
        part = 2 * part + place // step % 2
        step *= 2
    return part


def pair_plan(width, size):
    rows = []
    for place in range(width):
        lo, count, kept, steps, step = 0, width, [], [], 1
        while step <= width:
            count //= 2
            upper = place // step % 2
            start_at = lo + (1 - upper) * count
            if step == width:
                start_at, count = lo, 1
            steps.append(
                [
                    [c * width + start_at + i] + [c * many + start_at + i - base for base, many in kept]
                    for c in range(size)
                    for i in range(count)
                ]
            )
            lo += upper * count if step < width else 0
            kept.append((lo, count))
            step *= 2
        rows.append(steps)
    return rows


def pair_step(rows, scaled, received, plan, first, shift, nb, block, mode, other=None, rank_count=None):
    depth = rows.shape[1]
    group = scaled.shape[1]
    n = len(received)
    length = nb * block

    def body(plan_ref, row_ref, scaled_ref, *refs):
        both = scaled_ref[...].reshape(2 * group, depth)
        product = lax.dot_general(
            row_ref[...], both, (((1,), (1,)), ((), ())), preferred_element_type=jnp.float32
        )
        total = product[:, :group] + product[:, group:]
        for i in range(n):
            total = total + decode(refs[i])
        out_ref = refs[-1]
        if mode == "code":
            encode(total, out_ref)
        elif mode == "plain":
            out_ref[...] = total
        else:
            joined = total * refs[n][...]
            out_ref[0] = jnp.sum(joined.reshape(block // rank_count, rank_count, group), axis=1)

    def place_of(column):
        return lambda b, s: (s[first + b * (n + 1) + column] + (shift if column == 0 else 0), 0)

    in_specs = [
        pl.BlockSpec((block, depth), place_of(0)),
        pl.BlockSpec((2, group, depth), lambda b, s: (0, 0, 0), pipeline_mode=pl.Buffered(1)),
    ]
    for i in range(n):
        in_specs.append(pl.BlockSpec((block + scale_rows, group), place_of(1 + i)))
    operands = [rows, scaled, *received]
    if mode == "code":
        out_shape = jax.ShapeDtypeStruct((nb * (block + scale_rows), group), jnp.bfloat16)
        out_spec = pl.BlockSpec((block + scale_rows, group), lambda b, s: (b, 0))
    elif mode == "plain":
        out_shape = jax.ShapeDtypeStruct((length, group), jnp.float32)
        out_spec = pl.BlockSpec((block, group), lambda b, s: (b, 0))
    else:
        other, at = other
        in_specs.append(pl.BlockSpec((block, group), lambda b, s: (at + b, 0)))
        operands.append(other)
        out_shape = jax.ShapeDtypeStruct((nb, block // rank_count, group), jnp.float32)
        out_spec = pl.BlockSpec((1, block // rank_count, group), lambda b, s: (b, 0, 0))
    return pl.pallas_call(
        body,
        out_shape=out_shape,
        grid_spec=pltpu.PrefetchScalarGridSpec(
            num_scalar_prefetch=1, grid=(nb,), in_specs=in_specs, out_specs=out_spec
        ),
        compiler_params=pltpu.CompilerParams(dimension_semantics=("arbitrary",)),
        cost_estimate=pl.CostEstimate(
            flops=4 * length * depth * group,
            transcendentals=2 * length * group,
            bytes_accessed=length * depth * 2 + 2 * group * depth * 2,
        ),
    )(plan, *operands)


def reduce_pairs(members, rows, scaled, plan, firsts, block, width, other=None, rank_count=None):
    received = []
    step, nb, shift = 1, len(members) * width, members[0] * width
    while step < width:
        nb //= 2
        code = pair_step(rows, scaled, received, plan, firsts[len(received)], shift, nb, block, "code")
        pairs = [(i, i ^ step) for i in range(width)]
        received = received + [in_vmem(lax.ppermute(code, "width", pairs))]
        step *= 2
    mode = "plain" if other is None else "joined"
    return pair_step(
        rows, scaled, received, plan, firsts[len(received)], shift, nb, block, mode, other, rank_count
    )


def assemble(batches, plan, first):
    width = len(batches[0])
    arrays = [array for batch in batches for array in batch]
    total = sum(batch[0].shape[0] for batch in batches)

    def body(plan_ref, *refs):
        out_ref = refs[-1]
        base = 0
        for b, batch in enumerate(batches):
            size = batch[0].shape[0]
            for x in range(width):
                for c in range(size):
                    out_ref[base + c, pl.ds(plan_ref[first + x], 1)] = refs[b * width + x][pl.ds(c, 1)]
            base += size

    return pl.pallas_call(
        body,
        out_shape=jax.ShapeDtypeStruct((total, width) + arrays[0].shape[1:], jnp.float32),
        in_specs=[pl.BlockSpec(memory_space=pltpu.SMEM)] + [pl.BlockSpec(memory_space=pltpu.VMEM)] * len(arrays),
        out_specs=pl.BlockSpec(memory_space=pltpu.VMEM),
        name="assemble",
    )(plan, *arrays)


def in_vmem(x):
    return pltpu.with_memory_space_constraint(x, pltpu.VMEM)


def gather_rotate(own, basis, plan, width):
    even, odd = swap_pairs(width)
    count = 1 + len(line_sources(width, 0))
    send_even = send_odd = own
    acc = rotate_step(None, 0, [own], basis, plan, count, width == 1)
    done = 1
    for distance in range(1, max(width - 1, 2) if width > 1 else 1):
        got = [lax.ppermute(send_even, "width", even)]
        if width > 2:
            got.append(lax.ppermute(send_odd, "width", odd))
            send_even, send_odd = got[1], got[0]
            if distance == width - 2:
                got.append(lax.ppermute(own, "width", far_pairs(width)))
        last = done + len(got) == count
        acc = rotate_step(acc, done, [in_vmem(x) for x in got], basis, plan, count, last)
        done += len(got)
    return acc


def scaled_group(rotated, squares, code, place, total_tokens):
    query_count, token_count = lax.axis_size("query"), lax.axis_size("token")
    codes, total = [], squares
    for by in range(1, query_count):
        shifted = shift_pairs(query_count, by)
        codes.append(in_vmem(lax.ppermute(code, "query", shifted)))
        total = total + lax.ppermute(squares, "query", shifted)
    sums = [total] + [lax.ppermute(total, "token", shift_pairs(token_count, by)) for by in range(1, token_count)]
    return split_scaled(rotated, codes, sums, place, total_tokens)


def compute(layer_inputs, out_grads, basis_in, basis_out, query_in, query_out):
    width = lax.axis_size("width")
    place = lax.axis_index("width")
    total_tokens = layer_inputs.shape[0] * lax.axis_size("token") * lax.axis_size("query")
    queries, rank_count, width_cols = query_in.shape
    rows_in = query_in.reshape(-1, width_cols)
    rows_out = query_out.reshape(-1, width_cols)
    block = rows_in.shape[0] // (chunks * width)

    depth = layer_inputs.shape[1]
    table = rotate_plan(width, depth // min(basis_block, depth))
    firsts = {}
    for size in sorted({len(members) for members in groups_in + groups_out}):
        firsts[size] = []
        for step in range(len(pair_plan(width, size)[0])):
            firsts[size].append(len(table[0]))
            for at, steps in enumerate(pair_plan(width, size)):
                table[at] += [number for entry in steps[step] for number in entry]
    parts_at = len(table[0])
    for at in range(width):
        table[at] += [mirror(at ^ x, width) for x in range(width)]
    plan = lax.dynamic_index_in_dim(jnp.asarray(table, jnp.int32), place, keepdims=False)
    query_place = lax.axis_index("query").astype(jnp.int32)[None]

    got_in = gather_rotate(layer_inputs, basis_in, plan, width)
    got_out = gather_rotate(out_grads, basis_out, plan, width)
    scaled_in = scaled_group(*got_in, query_place, total_tokens)
    scaled_out = scaled_group(*got_out, query_place, total_tokens)

    found = {}
    for members in groups_in:
        pairs = reduce_pairs(members, rows_in, scaled_in, plan, firsts[len(members)], block, width)
        found.update({c: (pairs, i) for i, c in enumerate(members)})
    batches = []
    for members in groups_out:
        own = reduce_pairs(
            members, rows_out, scaled_out, plan, firsts[len(members)], block, width, found[members[0]], rank_count
        )
        batches.append(own)
    own = jnp.concatenate(batches, axis=0)
    far = [lax.ppermute(own, "width", [(i, i ^ x) for i in range(width)]) for x in range(1, width)]
    scores = assemble([[own] + far], plan, parts_at)
    return scores.reshape(queries, scores.shape[-1])


def solution(mesh):
    return jax.shard_map(
        compute,
        mesh=mesh,
        in_specs=(
            P(("token", "query"), "width"),
            P(("token", "query"), "width"),
            P(None, "width"),
            P(None, "width"),
            P("query", None, "width"),
            P("query", None, "width"),
        ),
        out_specs=P("query", "token"),
        check_vma=False,
    )
```
